32 devices in a mesh: slab: 4 (over y, x), leaf: 8 (over z, core).
Axes of the slice: x: 2, y: 2, z: 4, core: 2. Of those that a mesh axis runs over, the one named last changes fastest.
Arguments:
- right_sides: bfloat16 [32, 131072], P(None, ('slab', 'leaf')), may hold values from -6 to 6
- left_sides: bfloat16 [32, 131072], P(None, ('slab', 'leaf')), may hold values from -6 to 6
- near_blocks: bfloat16 [1024, 8, 128, 128], P(('slab', 'leaf')), may hold values from -0.1875 to 0.1875
- near_columns: int32 [1024, 8], P(('slab', 'leaf')), may hold values from 0 to 1023, as said below
- cluster_points: int32 [1024], P(('slab', 'leaf')), may hold values from 64 to 128, as said below
- leaf_basis: bfloat16 [1024, 64, 128], P(('slab', 'leaf')), may hold values from -0.5 to 0.5
- transfer: float32 [1024, 64, 128], P(('slab', 'leaf')), may hold values from -0.625 to 0.625
- far_parents: int32 [32, 24], P(('slab', 'leaf')), may hold values from 0 to 31, as said below
- far_count: int32 [32], P(('slab', 'leaf')), may hold values from 12 to 24, as said below
- coupling: float32 [32, 24, 128, 128], P(('slab', 'leaf')), may hold values from -0.375 to 0.375
- slab_transfer: float32 [32, 128, 128], P(('slab', 'leaf')), may hold values from -0.75 to 0.75
- apex_coupling: float32 [4, 4, 128, 128], replicated, may hold values from -0.75 to 0.75
Outputs:
- product: float32 [32, 131072], P(None, ('slab', 'leaf'))
- adjoint_product: float32 [32, 131072], P(None, ('slab', 'leaf'))
The draws below stay inside these ranges and needn't reach their ends.
Inputs may be any that keep to these rules, and one draw needn't show every extreme that they name: `near_columns`: row i holds 8 different clusters, i among them, all inside the window of 9 consecutive clusters centred on i, moved inward where it would pass an end of 0 to 1023. `cluster_points`: some cluster has exactly 128 points and some exactly 64. `far_parents`: row p holds 24 different parents, none equal to p; only the first far_count[p] are used. `far_count`: some parent uses all 24 slots and some exactly 12.
All inputs are finite; a program needn't handle non-finite values.
Results may differ from the reference program's by a relative error of at most 0.0024.
Values may be sent and summed in bfloat16 or wider, within the bound.
A program may use at most 128 MiB of HBM per device.

```python
import jax
import jax.numpy as jnp
from jax import lax

B = 128
R = 32
K = 64
K2 = 128
K3 = 128
NN = 8
HW = 4
CL = 32
PARENTS = 32
NF = 24
SLABS = 4
PER_SLAB = 8
NC = 1024
N = 131072


def draw_near_columns(key, part):
    window = 2 * HW + 1
    row_index = jnp.arange(NC, dtype=jnp.int32)
    window_start = jnp.clip(row_index - HW, 0, NC - window)
    scores = jax.random.randint(key, (NC, window), 0, 1 << 16, dtype=jnp.int32) * window + jnp.arange(window, dtype=jnp.int32)[None, :]
    own_slot = (row_index - window_start)[:, None] == jnp.arange(window, dtype=jnp.int32)[None, :]
    scores = jnp.where(own_slot, -1, scores)
    ranking = jnp.argsort(scores, axis=1)[:, :NN].astype(jnp.int32)
    return (window_start[:, None] + ranking).astype(jnp.int32)


def draw_cluster_points(key, part):
    values = jax.random.randint(key, (NC,), B // 2, B + 1, dtype=jnp.int32)
    top_slot = jax.random.randint(jax.random.fold_in(key, 1), (), 0, NC, dtype=jnp.int32)
    low_slot = (top_slot + 1) % NC
    return values.at[top_slot].set(B).at[low_slot].set(B // 2).astype(jnp.int32)


def draw_far_parents(key, part):
    scores = jax.random.randint(key, (PARENTS, PARENTS), 0, 1 << 20, dtype=jnp.int32) * PARENTS + jnp.arange(PARENTS, dtype=jnp.int32)[None, :]
    scores = jnp.where(jnp.eye(PARENTS, dtype=jnp.bool_), 1 << 30, scores)
    return jnp.argsort(scores, axis=1)[:, :NF].astype(jnp.int32)


def draw_far_count(key, part):
    values = jax.random.randint(key, (PARENTS,), NF // 2, NF + 1, dtype=jnp.int32)
    top_slot = jax.random.randint(jax.random.fold_in(key, 2), (), 0, PARENTS, dtype=jnp.int32)
    low_slot = (top_slot + 1) % PARENTS
    return values.at[top_slot].set(NF).at[low_slot].set(NF // 2).astype(jnp.int32)


def level_of(stream_key, dims, cuts, smallest, high):
    def one(axis_at, shards_of):
        heights = jax.random.uniform(jax.random.fold_in(jax.random.fold_in(stream_key, 6), axis_at), (shards_of,), jnp.float32, smallest / len(cuts), high / len(cuts))
        return jnp.repeat(jnp.exp(heights), dims[axis_at] // shards_of).reshape((-1,) + (1,) * (len(dims) - axis_at - 1))

    gain = one(*cuts[0])
    for cut in cuts[1:]:
        gain = gain * one(*cut)
    return gain


def noise(stream_key, dims, scale, most, cuts=(), kind=jnp.bfloat16):
    gain = level_of(stream_key, dims, cuts, -0.22, 0.18) if cuts else 1.0
    array = jax.random.normal(stream_key, dims, jnp.float32) * scale * gain
    return jnp.minimum(jnp.maximum(array, -most), most).astype(kind)


def setup_inputs(seed: int = 0) -> dict:
    seeds = jax.random.split(jax.random.key(seed), 13)
    return {
        "right_sides": noise(seeds[0], (R, N), 1.0, 6.0, ((1, 32),)),
        "left_sides": noise(seeds[1], (R, N), 1.0, 6.0, ((1, 32),)),
        "near_blocks": noise(seeds[2], (NC, NN, B, B), (B * NN) ** -0.5, 0.1875, ((0, 32),)),
        "near_columns": draw_near_columns(jax.random.fold_in(seeds[12], 71), 0),
        "cluster_points": draw_cluster_points(jax.random.fold_in(seeds[12], 71), 0),
        "leaf_basis": noise(seeds[5], (NC, K, B), B ** -0.5, 0.5, ((0, 32),)),
        "transfer": noise(seeds[6], (NC, K, K2), ((CL * K * K2) ** -0.25), 0.625, ((0, 32),), jnp.float32),
        "far_parents": draw_far_parents(jax.random.fold_in(seeds[12], 71), 0),
        "far_count": draw_far_count(jax.random.fold_in(seeds[12], 71), 0),
        "coupling": noise(seeds[9], (PARENTS, NF, K2, K2), ((NF * K2 // 2) ** -0.5), 0.375, ((0, 32),), jnp.float32),
        "slab_transfer": noise(seeds[10], (PARENTS, K2, K3), ((PER_SLAB * K2 * K3) ** -0.25), 0.75, ((0, 32),), jnp.float32),
        "apex_coupling": noise(seeds[11], (SLABS, SLABS, K3, K3), (((SLABS - 1) * K3) ** -0.5), 0.75, (), jnp.float32),
    }


def reference(right_sides, left_sides, near_blocks, near_columns, cluster_points, leaf_basis, transfer, far_parents, far_count, coupling, slab_transfer, apex_coupling):
    uppermost_level = lax.Precision.HIGHEST
    point_mask = jnp.arange(B, dtype=jnp.int32)[None, :] < cluster_points[:, None]
    zero_bf = jnp.zeros((), jnp.bfloat16)
    masked_right = jnp.where(point_mask[None], right_sides.reshape(R, NC, B), zero_bf)
    masked_left = jnp.where(point_mask[None], left_sides.reshape(R, NC, B), zero_bf)
    group_blocks = near_blocks.reshape(PARENTS, CL, NN, B, B)
    group_columns = near_columns.reshape(PARENTS, CL, NN)
    group_left = jnp.transpose(masked_left.reshape(R, PARENTS, CL, B), (1, 0, 2, 3))

    def near_forward(pieces):
        blocks, columns = pieces
        picked = jnp.take(masked_right, columns, axis=1).astype(jnp.float32)
        return jnp.einsum("csab,rcsb->rca", blocks.astype(jnp.float32), picked, precision=uppermost_level)

    near_out = lax.map(near_forward, (group_blocks, group_columns))
    near_out = jnp.transpose(near_out, (1, 0, 2, 3)).reshape(R, NC, B)

    def near_transposed(total, pieces):
        blocks, columns, lefts = pieces
        contrib = jnp.einsum("csab,rca->csrb", blocks.astype(jnp.float32), lefts.astype(jnp.float32), precision=uppermost_level)
        total = total.at[columns.reshape(-1)].add(contrib.reshape(CL * NN, R, B))
        return total, None

    near_back, _ = lax.scan(near_transposed, jnp.zeros((NC, R, B), jnp.float32), (group_blocks, group_columns, group_left))
    near_back = jnp.transpose(near_back, (1, 0, 2))

    basis_wide = leaf_basis.astype(jnp.float32)
    leaf_right = jnp.einsum("ckb,rcb->ckr", basis_wide, masked_right.astype(jnp.float32), precision=uppermost_level)
    leaf_left = jnp.einsum("ckb,rcb->ckr", basis_wide, masked_left.astype(jnp.float32), precision=uppermost_level)
    parent_right = jnp.einsum("ckq,ckr->cqr", transfer, leaf_right, precision=uppermost_level).reshape(PARENTS, CL, K2, R).sum(axis=1)
    parent_left = jnp.einsum("ckq,ckr->cqr", transfer, leaf_left, precision=uppermost_level).reshape(PARENTS, CL, K2, R).sum(axis=1)

    live = (jnp.arange(NF, dtype=jnp.int32)[None, :] < far_count[:, None]).astype(jnp.float32)
    far_right = jnp.einsum("pf,pfab,pfbr->par", live, coupling, parent_right[far_parents], precision=uppermost_level)
    outward = jnp.einsum("pf,pfab,par->pfbr", live, coupling, parent_left, precision=uppermost_level)
    far_left = jnp.zeros((PARENTS, K2, R), jnp.float32).at[far_parents.reshape(-1)].add(outward.reshape(PARENTS * NF, K2, R))

    slab_right = jnp.einsum("pqt,pqr->ptr", slab_transfer, parent_right, precision=uppermost_level).reshape(SLABS, PER_SLAB, K3, R).sum(axis=1)
    slab_left_factor = jnp.einsum("pqt,pqr->ptr", slab_transfer, parent_left, precision=uppermost_level).reshape(SLABS, PER_SLAB, K3, R).sum(axis=1)
    remaining_slabs = 1.0 - jnp.eye(SLABS, dtype=jnp.float32)
    apex_right = jnp.einsum("st,stab,tbr->sar", remaining_slabs, apex_coupling, slab_right, precision=uppermost_level)
    apex_left = jnp.einsum("uc,ucnh,unx->chx", remaining_slabs, apex_coupling, slab_left_factor, precision=uppermost_level)
    hat_right = far_right + jnp.einsum("pqt,ptr->pqr", slab_transfer, jnp.repeat(apex_right, PER_SLAB, axis=0), precision=uppermost_level)
    hat_left = far_left + jnp.einsum("pqt,ptr->pqr", slab_transfer, jnp.repeat(apex_left, PER_SLAB, axis=0), precision=uppermost_level)

    down_right = jnp.einsum("ckq,cqr->ckr", transfer, jnp.repeat(hat_right, CL, axis=0), precision=uppermost_level).astype(jnp.bfloat16)
    down_left = jnp.einsum("ckq,cqr->ckr", transfer, jnp.repeat(hat_left, CL, axis=0), precision=uppermost_level).astype(jnp.bfloat16)
    far_out = jnp.einsum("ckb,ckr->rcb", basis_wide, down_right.astype(jnp.float32), precision=uppermost_level)
    far_back = jnp.einsum("ckb,ckr->rcb", basis_wide, down_left.astype(jnp.float32), precision=uppermost_level)
    zero_wide = jnp.zeros((), jnp.float32)
    product = jnp.where(point_mask[None], near_out + far_out, zero_wide).reshape(R, N)
    adjoint_product = jnp.where(point_mask[None], near_back + far_back, zero_wide).reshape(R, N)
    return product, adjoint_product
```

```python
import functools

import jax
import jax.numpy as jnp
from jax import lax
from jax.experimental import pallas as pl
from jax.experimental.pallas import tpu as pltpu
from jax.sharding import PartitionSpec as P

B = 128
HW = 4
BF = jnp.bfloat16
F32 = jnp.float32
MESH = pl.DeviceIdType.MESH


def nt(a, b):
    return lax.dot_general(a, b, (((1,), (1,)), ((), ())), preferred_element_type=F32)


def nn(a, b):
    return lax.dot_general(a, b, (((1,), (0,)), ((), ())), preferred_element_type=F32)


def split(x):
    high = x.astype(BF)
    return high, (x - high.astype(F32)).astype(BF)


def three(a, b, product):
    rows = a.shape[0]
    ah, al = split(a)
    bh, bl = split(b)
    both = product(jnp.concatenate([ah, al], axis=0), bh)
    return both[:rows] + both[rows:] + product(ah, bl)


def kernel(
    slabs,
    leaves,
    points_s,
    columns_s,
    inverse_s,
    targets_s,
    count_s,
    far_inverse_s,
    right_h,
    left_h,
    basis_h,
    transfer_h,
    lift_h,
    coupling_h,
    apex_h,
    near_h,
    product_ref,
    adjoint_ref,
    right_v,
    left_v,
    basis_v,
    transfer_v,
    lift_v,
    coupling_v,
    apex_row_v,
    apex_col_v,
    near_v,
    ext_v,
    masked_left_v,
    collected_v,
    near_out_v,
    edge_out_v,
    edge_in_v,
    share_v,
    share_in_v,
    slab_v,
    parents_v,
    outward_v,
    arrived_v,
    down_v,
    in_sem,
    halo_send,
    halo_recv,
    edge_send,
    edge_recv,
    share_send,
    share_recv,
    slab_send,
    slab_recv,
    parent_send,
    parent_recv,
    out_send,
    out_recv,
):
    rhs = right_h.shape[0]
    clusters, slots = near_v.shape[:2]
    rank = basis_v.shape[1]
    far_slots = coupling_v.shape[0]
    devices = slabs * leaves
    width = 2 * HW + 1
    my_slab = lax.axis_index("slab")
    my_leaf = lax.axis_index("leaf")
    me = my_slab * leaves + my_leaf
    first = 1 - (me + devices - 1) // devices
    last = (me + 1) // devices

    def place(d):
        return (d // leaves, d % leaves)

    ext_v[0:HW] = jnp.zeros((HW, rhs, B), BF)
    ext_v[clusters + HW :] = jnp.zeros((HW, rhs, B), BF)
    edge_in_v[...] = jnp.zeros_like(edge_in_v)

    inputs = [
        pltpu.make_async_copy(src, dst, in_sem.at[i])
        for i, (src, dst) in enumerate(
            [
                (right_h, right_v),
                (left_h, left_v),
                (basis_h, basis_v),
                (transfer_h, transfer_v),
                (lift_h, lift_v),
                (coupling_h, coupling_v),
                (near_h, near_v),
                (apex_h.at[my_slab], apex_row_v),
                (apex_h.at[:, my_slab], apex_col_v),
            ]
        )
    ]
    for copy in inputs:
        copy.start()

    barrier = pltpu.get_barrier_semaphore()

    def greet(k, _):
        pl.semaphore_signal(
            barrier, inc=1, device_id=place((me + k) % devices), device_id_type=MESH
        )
        return 0

    lax.fori_loop(1, devices, greet, 0)

    collected_v[...] = jnp.zeros_like(collected_v)
    for copy in inputs[:4]:
        copy.wait()

    lane = lax.broadcasted_iota(jnp.int32, (rhs, B), 1)

    def window(c):
        return pl.ds(pl.multiple_of(c * B, B), B)

    def mask_of(c):
        return jnp.where(lane < points_s[c], 1.0, 0.0)

    def leaf_step(c, total):
        mask = mask_of(c).astype(BF)
        r = right_v[:, window(c)] * mask
        l = left_v[:, window(c)] * mask
        ext_v[c + HW] = r
        masked_left_v[c] = l
        leaf = nt(jnp.concatenate([r, l], axis=0), basis_v[c])
        return total + three(leaf, transfer_v[c], nn)

    unroll = 4

    def leaf_group(g, total):
        for u in range(unroll):
            total = leaf_step(g * unroll + u, total)
        return total

    parent = lax.fori_loop(
        0, clusters // unroll, leaf_group, jnp.zeros((2 * rhs, transfer_v.shape[2]), F32)
    )

    parents_v[me] = parent[:rhs].astype(BF)
    inputs[4].wait()
    share = three(parent, lift_v[...], nn)
    chunk = share_v.shape[1]
    for j in range(leaves):
        share_v[j] = share[j * chunk : (j + 1) * chunk]

    pl.semaphore_wait(barrier, devices - 1)

    def halo_copy(to_next):
        where = me + 1 if to_next else me - 1
        src = clusters if to_next else HW
        dst = 0 if to_next else clusters + HW
        i = 0 if to_next else 1
        return pltpu.make_async_remote_copy(
            src_ref=ext_v.at[pl.ds(src, HW)],
            dst_ref=ext_v.at[pl.ds(dst, HW)],
            send_sem=halo_send.at[i],
            recv_sem=halo_recv.at[i],
            device_id=place(where),
            device_id_type=MESH,
        )

    def share_copy(k):
        peer = (my_leaf + k) % leaves
        return pltpu.make_async_remote_copy(
            src_ref=share_v.at[peer],
            dst_ref=share_in_v.at[my_leaf],
            send_sem=share_send.at[k],
            recv_sem=share_recv.at[k],
            device_id=(my_slab, peer),
            device_id_type=MESH,
        )

    def share_arrival(k):
        peer = (my_leaf + leaves - k) % leaves
        return pltpu.make_async_remote_copy(
            src_ref=share_v.at[my_leaf],
            dst_ref=share_in_v.at[peer],
            send_sem=share_send.at[k],
            recv_sem=share_recv.at[k],
            device_id=(my_slab, peer),
            device_id_type=MESH,
        )

    def wide_copy(k, src, dst, send, recv, spread):
        peer = (me + k) % devices
        return pltpu.make_async_remote_copy(
            src_ref=src.at[peer if spread else me],
            dst_ref=dst.at[me],
            send_sem=send.at[k],
            recv_sem=recv.at[k],
            device_id=place(peer),
            device_id_type=MESH,
        )

    def wide_arrival(k, src, dst, send, recv):
        peer = (me + devices - k) % devices
        return pltpu.make_async_remote_copy(
            src_ref=src.at[me],
            dst_ref=dst.at[peer],
            send_sem=send.at[k],
            recv_sem=recv.at[k],
            device_id=place(peer),
            device_id_type=MESH,
        )

    def loop(low, high, act):
        def step(k, carry):
            act(k)
            return carry

        lax.fori_loop(low, high, step, 0)

    loop(1, leaves, lambda k: share_copy(k).start())
    share_in_v[my_leaf] = share_v[my_leaf]

    @pl.when(me < devices - 1)
    def _():
        halo_copy(True).start()

    @pl.when(me > 0)
    def _():
        halo_copy(False).start()

    inputs[5].wait()
    lh, ll = split(parent[rhs:])
    left_both = jnp.concatenate([lh, ll], axis=0)

    def outward(q):
        f = far_inverse_s[q]
        live = jnp.where(f >= 0, 1.0, 0.0)
        ch, cl = split(coupling_v[jnp.maximum(f, 0)])
        both = nn(left_both, ch)
        term = both[:rhs] + both[rhs:] + nn(lh, cl)
        outward_v[q] = (term * live).astype(BF)

    def outward_group(g):
        for u in range(unroll):
            outward(g * unroll + u)

    loop(0, devices // unroll, outward_group)
    arrived_v[me] = jnp.zeros((rhs, arrived_v.shape[2]), BF)

    loop(1, leaves, lambda k: share_arrival(k).wait_recv())
    total = share_in_v[0]
    for j in range(1, leaves):
        total = total + share_in_v[j]
    slab_v[me] = total

    loop(1, devices, lambda k: wide_copy(k, slab_v, slab_v, slab_send, slab_recv, False).start())
    loop(
        1,
        devices,
        lambda k: wide_copy(k, parents_v, parents_v, parent_send, parent_recv, False).start(),
    )
    loop(
        1,
        devices,
        lambda k: wide_copy(k, outward_v, arrived_v, out_send, out_recv, True).start(),
    )

    inputs[6].wait()

    def near_back(i, e0):
        left = masked_left_v[i]
        for w in range(width):
            s = inverse_s[i * width + w]
            live = jnp.where(s >= 0, 1.0, 0.0)
            term = nn(left, near_v[i, jnp.maximum(s, 0)])
            collected_v[e0 + w] += term * live

    def near_forward(i):
        total = None
        for s in range(slots):
            term = nt(ext_v[columns_s[i * slots + s]], near_v[i, s])
            total = term if total is None else total + term
        near_out_v[i] = total

    for i in range(HW):
        near_back(i, i + first * (HW - i))
    for i in range(clusters - HW, clusters):
        near_back(i, i - last * (i - (clusters - HW - 1)))

    edge_out_v[0] = collected_v[0:HW].astype(BF)
    edge_out_v[1] = collected_v[clusters + HW :].astype(BF)

    def edge_copy(to_next):
        i = 1 if to_next else 0
        return pltpu.make_async_remote_copy(
            src_ref=edge_out_v.at[i],
            dst_ref=edge_in_v.at[i],
            send_sem=edge_send.at[i],
            recv_sem=edge_recv.at[i],
            device_id=place(me + 1 if to_next else me - 1),
            device_id_type=MESH,
        )

    @pl.when(me < devices - 1)
    def _():
        edge_copy(True).start()

    @pl.when(me > 0)
    def _():
        edge_copy(False).start()

    @pl.when(me > 0)
    def _():
        halo_copy(True).wait_recv()

    @pl.when(me < devices - 1)
    def _():
        halo_copy(False).wait_recv()

    for i in list(range(HW)) + list(range(clusters - HW, clusters)):
        near_forward(i)

    def middle(i):
        near_back(i, i)
        near_forward(i)

    loop(HW, clusters - HW, middle)

    @pl.when(me > 0)
    def _():
        edge_copy(True).wait_recv()

    @pl.when(me < devices - 1)
    def _():
        edge_copy(False).wait_recv()

    collected_v[HW : 2 * HW] += edge_in_v[1].astype(F32)
    collected_v[clusters : clusters + HW] += edge_in_v[0].astype(F32)

    loop(1, devices, lambda k: wide_arrival(k, slab_v, slab_v, slab_send, slab_recv).wait_recv())
    inputs[7].wait()
    inputs[8].wait()
    apex_right = jnp.zeros((rhs, lift_v.shape[1]), F32)
    apex_left = jnp.zeros((rhs, lift_v.shape[1]), F32)
    for t in range(slabs):
        other = jnp.where(my_slab == t, 0.0, 1.0)
        whole = jnp.concatenate([slab_v[t * leaves + j] for j in range(leaves)], axis=0)
        apex_right += other * three(whole[:rhs], apex_row_v[t], nt)
        apex_left += other * three(whole[rhs:], apex_col_v[t], nn)
    spread = three(jnp.concatenate([apex_right, apex_left], axis=0), lift_v[...], nt)

    loop(
        1,
        devices,
        lambda k: wide_arrival(k, parents_v, parents_v, parent_send, parent_recv).wait_recv(),
    )

    def far(f, total):
        live = jnp.where(f < count_s[0], 1.0, 0.0)
        ch, cl = split(coupling_v[f])
        chosen = parents_v[targets_s[f]]
        return total + live * (nt(chosen, ch) + nt(chosen, cl))

    def far_group(g, total):
        for u in range(unroll):
            total = far(g * unroll + u, total)
        return total

    far_right = lax.fori_loop(0, far_slots // unroll, far_group, spread[:rhs])

    loop(
        1, devices, lambda k: wide_arrival(k, outward_v, arrived_v, out_send, out_recv).wait_recv()
    )
    far_left = lax.fori_loop(
        0, devices, lambda d, total: total + arrived_v[d].astype(F32), spread[rhs:]
    )

    hat = jnp.concatenate([far_right, far_left], axis=0)
    hh, hl = split(hat)
    hat_both = jnp.concatenate([hh, hl], axis=0)

    def finish(c):
        th, tl = split(transfer_v[c])
        both = nt(hat_both, th)
        down = (both[: 2 * rhs] + both[2 * rhs :] + nt(hh, tl)).astype(BF)
        out = nn(down, basis_v[c])
        keep = lane < points_s[c]
        product_ref[:, window(c)] = jnp.where(keep, near_out_v[c] + out[:rhs], 0.0)
        adjoint_ref[:, window(c)] = jnp.where(keep, collected_v[c + HW] + out[rhs:], 0.0)

    def finish_group(g):
        for u in range(unroll):
            finish(g * unroll + u)

    loop(0, clusters // unroll, finish_group)

    loop(1, leaves, lambda k: share_copy(k).wait_send())
    loop(1, devices, lambda k: wide_copy(k, slab_v, slab_v, slab_send, slab_recv, False).wait_send())
    loop(
        1,
        devices,
        lambda k: wide_copy(k, parents_v, parents_v, parent_send, parent_recv, False).wait_send(),
    )
    loop(
        1,
        devices,
        lambda k: wide_copy(k, outward_v, arrived_v, out_send, out_recv, True).wait_send(),
    )

    @pl.when(me < devices - 1)
    def _():
        halo_copy(True).wait_send()
        edge_copy(True).wait_send()

    @pl.when(me > 0)
    def _():
        halo_copy(False).wait_send()
        edge_copy(False).wait_send()


def shards(
    right_sides,
    left_sides,
    near_blocks,
    near_columns,
    cluster_points,
    leaf_basis,
    transfer,
    far_parents,
    far_count,
    coupling,
    slab_transfer,
    apex_coupling,
):
    slabs, leaves = lax.axis_size("slab"), lax.axis_size("leaf")
    devices = slabs * leaves
    rhs, columns = right_sides.shape
    clusters, slots = near_columns.shape
    rank, k2 = transfer.shape[1:]
    k3 = slab_transfer.shape[2]
    far_slots = coupling.shape[1]
    width = 2 * HW + 1
    me = lax.axis_index(("slab", "leaf"))
    rows = me * clusters + jnp.arange(clusters, dtype=jnp.int32)
    start = jnp.clip(rows - HW, 0, devices * clusters - width)
    wanted = start[:, None] + jnp.arange(width, dtype=jnp.int32)[None, :]
    number = jnp.arange(1, slots + 1, dtype=jnp.int32)
    inverse = (
        jnp.sum(jnp.where(near_columns[:, None, :] == wanted[:, :, None], number, 0), axis=2) - 1
    )
    f_index = jnp.arange(far_slots, dtype=jnp.int32)
    hit = (far_parents[0][None, :] == jnp.arange(devices, dtype=jnp.int32)[:, None]) & (
        f_index < far_count[0]
    )[None, :]
    far_inverse = jnp.sum(jnp.where(hit, f_index + 1, 0), axis=1) - 1

    chunk = 2 * rhs // leaves
    smem = pl.BlockSpec(memory_space=pltpu.SMEM)
    hbm = pl.BlockSpec(memory_space=pl.ANY)
    vmem = pl.BlockSpec(memory_space=pltpu.VMEM)
    dma = pltpu.SemaphoreType.DMA
    out = jax.ShapeDtypeStruct((rhs, columns), F32)
    return pl.pallas_call(
        functools.partial(kernel, slabs, leaves),
        out_shape=(out, out),
        in_specs=[smem] * 6 + [hbm] * 8,
        out_specs=(vmem, vmem),
        scratch_shapes=[
            pltpu.VMEM((rhs, columns), BF),
            pltpu.VMEM((rhs, columns), BF),
            pltpu.VMEM(leaf_basis.shape, BF),
            pltpu.VMEM(transfer.shape, F32),
            pltpu.VMEM((k2, k3), F32),
            pltpu.VMEM(coupling.shape[1:], F32),
            pltpu.VMEM((slabs, k3, k3), F32),
            pltpu.VMEM((slabs, k3, k3), F32),
            pltpu.VMEM(near_blocks.shape, BF),
            pltpu.VMEM((clusters + 2 * HW, rhs, B), BF),
            pltpu.VMEM((clusters, rhs, B), BF),
            pltpu.VMEM((clusters + 2 * HW, rhs, B), F32),
            pltpu.VMEM((clusters, rhs, B), F32),
            pltpu.VMEM((2, HW, rhs, B), BF),
            pltpu.VMEM((2, HW, rhs, B), BF),
            pltpu.VMEM((leaves, chunk, k3), F32),
            pltpu.VMEM((leaves, chunk, k3), F32),
            pltpu.VMEM((devices, chunk, k3), F32),
            pltpu.VMEM((devices, rhs, k2), BF),
            pltpu.VMEM((devices, rhs, k2), BF),
            pltpu.VMEM((devices, rhs, k2), BF),
            pltpu.VMEM((2 * rhs, rank), BF),
            dma((9,)),
            dma((2,)),
            dma((2,)),
            dma((2,)),
            dma((2,)),
            dma((leaves,)),
            dma((leaves,)),
            dma((devices,)),
            dma((devices,)),
            dma((devices,)),
            dma((devices,)),
            dma((devices,)),
            dma((devices,)),
        ],
        compiler_params=pltpu.CompilerParams(
            collective_id=0, has_side_effects=True, vmem_limit_bytes=48 * 1024 * 1024
        ),
        name="h2_step",
    )(
        cluster_points,
        (near_columns - (me * clusters - HW)).reshape(-1),
        inverse.reshape(-1),
        far_parents[0],
        far_count,
        far_inverse,
        right_sides,
        left_sides,
        leaf_basis,
        transfer,
        slab_transfer[0],
        coupling[0],
        apex_coupling,
        near_blocks,
    )


def solution(mesh):
    return jax.shard_map(
        shards,
        mesh=mesh,
        in_specs=(
            P(None, ("slab", "leaf")),
            P(None, ("slab", "leaf")),
            P(("slab", "leaf"), None, None, None),
            P(("slab", "leaf"), None),
            P(("slab", "leaf")),
            P(("slab", "leaf"), None, None),
            P(("slab", "leaf"), None, None),
            P(("slab", "leaf"), None),
            P(("slab", "leaf")),
            P(("slab", "leaf"), None, None, None),
            P(("slab", "leaf"), None, None),
            P(),
        ),
        out_specs=(P(None, ("slab", "leaf")), P(None, ("slab", "leaf"))),
        check_vma=False,
    )
```

```python
import functools

import jax
import jax.numpy as jnp
from jax import lax
from jax.experimental import pallas as pl
from jax.experimental.pallas import tpu as pltpu
from jax.sharding import PartitionSpec as P

B = 128
HW = 4
BF = jnp.bfloat16
F32 = jnp.float32
MESH = pl.DeviceIdType.MESH


def nt(a, b):
    return lax.dot_general(a, b, (((1,), (1,)), ((), ())), preferred_element_type=F32)


def nn(a, b):
    return lax.dot_general(a, b, (((1,), (0,)), ((), ())), preferred_element_type=F32)


def split(x):
    high = x.astype(BF)
    return high, (x - high.astype(F32)).astype(BF)


def three(a, b, product):
    rows = a.shape[0]
    ah, al = split(a)
    bh, bl = split(b)
    both = product(jnp.concatenate([ah, al], axis=0), bh)
    return both[:rows] + both[rows:] + product(ah, bl)


def kernel(
    slabs,
    leaves,
    points_s,
    targets_s,
    count_s,
    columns_h,
    right_h,
    left_h,
    basis_h,
    transfer_h,
    lift_h,
    coupling_h,
    apex_h,
    near_h,
    product_ref,
    adjoint_ref,
    right_v,
    left_v,
    basis_v,
    transfer_v,
    lift_v,
    coupling_v,
    apex_row_v,
    apex_col_v,
    near_v,
    columns_v,
    table_v,
    far_table_v,
    table_s,
    far_table_s,
    ext_v,
    masked_left_v,
    collected_v,
    near_out_v,
    edge_out_v,
    edge_in_v,
    share_v,
    share_in_v,
    slab_v,
    parents_v,
    outward_v,
    arrived_v,
    down_v,
    in_sem,
    table_sem,
    halo_send,
    halo_recv,
    edge_send,
    edge_recv,
    share_send,
    share_recv,
    slab_send,
    slab_recv,
    parent_send,
    parent_recv,
    out_send,
    out_recv,
):
    rhs = right_h.shape[0]
    slots, clusters = columns_v.shape
    rank = basis_v.shape[1]
    far_slots = coupling_v.shape[0]
    devices = slabs * leaves
    width = 2 * HW + 1
    my_slab = lax.axis_index("slab")
    my_leaf = lax.axis_index("leaf")
    me = my_slab * leaves + my_leaf
    first = 1 - (me + devices - 1) // devices
    last = (me + 1) // devices

    def place(d):
        return (d // leaves, d % leaves)

    ext_v[0:HW] = jnp.zeros((HW, rhs, B), BF)
    ext_v[clusters + HW :] = jnp.zeros((HW, rhs, B), BF)
    edge_in_v[...] = jnp.zeros_like(edge_in_v)

    inputs = [
        pltpu.make_async_copy(src, dst, in_sem.at[i])
        for i, (src, dst) in enumerate(
            [
                (right_h, right_v),
                (left_h, left_v),
                (basis_h, basis_v),
                (transfer_h, transfer_v),
                (lift_h, lift_v),
                (coupling_h, coupling_v),
                (near_h, near_v.at[pl.ds(0, clusters * slots)]),
                (apex_h.at[my_slab], apex_row_v),
                (apex_h.at[:, my_slab], apex_col_v),
                (columns_h, columns_v),
            ]
        )
    ]
    inputs[9].start()
    for copy in inputs[:9]:
        copy.start()

    barrier = pltpu.get_barrier_semaphore()

    def greet(k, _):
        pl.semaphore_signal(
            barrier, inc=1, device_id=place((me + k) % devices), device_id_type=MESH
        )
        return 0

    lax.fori_loop(1, devices, greet, 0)

    collected_v[...] = jnp.zeros_like(collected_v)
    near_v[clusters * slots] = jnp.zeros((B, B), BF)

    inputs[9].wait()
    row = lax.broadcasted_iota(jnp.int32, (1, clusters), 1)
    opening = (
        row
        + first * jnp.maximum(HW - row, 0)
        - last * jnp.maximum(row - (clusters - HW - 1), 0)
    )
    spots = [columns_v[s : s + 1] - (me * clusters - HW) for s in range(slots)]
    for w in range(width):
        found = jnp.full((1, clusters), clusters * slots, jnp.int32)
        for s in range(slots):
            found = jnp.where(spots[s] == opening + w, row * slots + s, found)
        table_v[w : w + 1] = found
    for s in range(slots):
        table_v[width + s : width + s + 1] = jnp.clip(spots[s], 0, clusters + 2 * HW - 1)
    owner = lax.broadcasted_iota(jnp.int32, (1, devices), 1)
    found = jnp.full((1, devices), -1, jnp.int32)
    for f in range(far_slots):
        target = jnp.where(f < count_s[0], targets_s[f], -1)
        found = jnp.where(owner == target, f, found)
    far_table_v[0:1] = found
    tables = [
        pltpu.make_async_copy(table_v, table_s, table_sem.at[0]),
        pltpu.make_async_copy(far_table_v, far_table_s, table_sem.at[1]),
    ]
    for copy in tables:
        copy.start()

    for copy in inputs[:4]:
        copy.wait()

    lane = lax.broadcasted_iota(jnp.int32, (rhs, B), 1)

    def window(c):
        return pl.ds(pl.multiple_of(c * B, B), B)

    def mask_of(c):
        return jnp.where(lane < points_s[c], 1.0, 0.0)

    def leaf_step(c, total):
        mask = mask_of(c).astype(BF)
        r = right_v[:, window(c)] * mask
        l = left_v[:, window(c)] * mask
        ext_v[c + HW] = r
        masked_left_v[c] = l
        leaf = nt(jnp.concatenate([r, l], axis=0), basis_v[c])
        return total + three(leaf, transfer_v[c], nn)

    unroll = 4

    def leaf_group(g, total):
        for u in range(unroll):
            total = leaf_step(g * unroll + u, total)
        return total

    parent = lax.fori_loop(
        0, clusters // unroll, leaf_group, jnp.zeros((2 * rhs, transfer_v.shape[2]), F32)
    )

    parents_v[me] = parent[:rhs].astype(BF)
    inputs[4].wait()
    share = three(parent, lift_v[...], nn)
    chunk = share_v.shape[1]
    for j in range(leaves):
        share_v[j] = share[j * chunk : (j + 1) * chunk]

    pl.semaphore_wait(barrier, devices - 1)

    def halo_copy(to_next):
        where = me + 1 if to_next else me - 1
        src = clusters if to_next else HW
        dst = 0 if to_next else clusters + HW
        i = 0 if to_next else 1
        return pltpu.make_async_remote_copy(
            src_ref=ext_v.at[pl.ds(src, HW)],
            dst_ref=ext_v.at[pl.ds(dst, HW)],
            send_sem=halo_send.at[i],
            recv_sem=halo_recv.at[i],
            device_id=place(where),
            device_id_type=MESH,
        )

    def share_copy(k):
        peer = (my_leaf + k) % leaves
        return pltpu.make_async_remote_copy(
            src_ref=share_v.at[peer],
            dst_ref=share_in_v.at[my_leaf],
            send_sem=share_send.at[k],
            recv_sem=share_recv.at[k],
            device_id=(my_slab, peer),
            device_id_type=MESH,
        )

    def share_arrival(k):
        peer = (my_leaf + leaves - k) % leaves
        return pltpu.make_async_remote_copy(
            src_ref=share_v.at[my_leaf],
            dst_ref=share_in_v.at[peer],
            send_sem=share_send.at[k],
            recv_sem=share_recv.at[k],
            device_id=(my_slab, peer),
            device_id_type=MESH,
        )

    def wide_copy(k, src, dst, send, recv, spread):
        peer = (me + k) % devices
        return pltpu.make_async_remote_copy(
            src_ref=src.at[peer if spread else me],
            dst_ref=dst.at[me],
            send_sem=send.at[k],
            recv_sem=recv.at[k],
            device_id=place(peer),
            device_id_type=MESH,
        )

    def wide_arrival(k, src, dst, send, recv):
        peer = (me + devices - k) % devices
        return pltpu.make_async_remote_copy(
            src_ref=src.at[me],
            dst_ref=dst.at[peer],
            send_sem=send.at[k],
            recv_sem=recv.at[k],
            device_id=place(peer),
            device_id_type=MESH,
        )

    def loop(low, high, act):
        def step(k, carry):
            act(k)
            return carry

        lax.fori_loop(low, high, step, 0)

    loop(1, leaves, lambda k: share_copy(k).start())
    share_in_v[my_leaf] = share_v[my_leaf]

    @pl.when(me < devices - 1)
    def _():
        halo_copy(True).start()

    @pl.when(me > 0)
    def _():
        halo_copy(False).start()

    inputs[5].wait()
    for copy in tables:
        copy.wait()
    lh, ll = split(parent[rhs:])
    left_both = jnp.concatenate([lh, ll], axis=0)

    def outward(q):
        f = far_table_s[0, q]
        live = jnp.where(f >= 0, 1.0, 0.0)
        ch, cl = split(coupling_v[jnp.maximum(f, 0)])
        both = nn(left_both, ch)
        term = both[:rhs] + both[rhs:] + nn(lh, cl)
        outward_v[q] = (term * live).astype(BF)

    def outward_group(g):
        for u in range(unroll):
            outward(g * unroll + u)

    loop(0, devices // unroll, outward_group)
    arrived_v[me] = jnp.zeros((rhs, arrived_v.shape[2]), BF)

    loop(1, leaves, lambda k: share_arrival(k).wait_recv())
    total = share_in_v[0]
    for j in range(1, leaves):
        total = total + share_in_v[j]
    slab_v[me] = total

    loop(1, devices, lambda k: wide_copy(k, slab_v, slab_v, slab_send, slab_recv, False).start())
    loop(
        1,
        devices,
        lambda k: wide_copy(k, parents_v, parents_v, parent_send, parent_recv, False).start(),
    )
    loop(
        1,
        devices,
        lambda k: wide_copy(k, outward_v, arrived_v, out_send, out_recv, True).start(),
    )

    inputs[6].wait()

    def near_back(i, e0):
        left = masked_left_v[i]
        for w in range(width):
            collected_v[e0 + w] += nn(left, near_v[table_s[w, i]])

    def near_forward(i):
        blocks = jnp.concatenate([near_v[i * slots + s] for s in range(slots)], axis=1)
        picked = jnp.concatenate([ext_v[table_s[width + s, i]] for s in range(slots)], axis=1)
        near_out_v[i] = nt(picked, blocks)

    for i in range(HW):
        near_back(i, i + first * (HW - i))
    for i in range(clusters - HW, clusters):
        near_back(i, i - last * (i - (clusters - HW - 1)))

    edge_out_v[0] = collected_v[0:HW].astype(BF)
    edge_out_v[1] = collected_v[clusters + HW :].astype(BF)

    def edge_copy(to_next):
        i = 1 if to_next else 0
        return pltpu.make_async_remote_copy(
            src_ref=edge_out_v.at[i],
            dst_ref=edge_in_v.at[i],
            send_sem=edge_send.at[i],
            recv_sem=edge_recv.at[i],
            device_id=place(me + 1 if to_next else me - 1),
            device_id_type=MESH,
        )

    @pl.when(me < devices - 1)
    def _():
        edge_copy(True).start()

    @pl.when(me > 0)
    def _():
        edge_copy(False).start()

    @pl.when(me > 0)
    def _():
        halo_copy(True).wait_recv()

    @pl.when(me < devices - 1)
    def _():
        halo_copy(False).wait_recv()

    for i in list(range(HW)) + list(range(clusters - HW, clusters)):
        near_forward(i)

    def middle(g):
        i = HW + g * HW
        lefts = [masked_left_v[i + u] for u in range(HW)]
        for e in range(width + HW - 1):
            rows = [u for u in range(HW) if 0 <= e - u < width]
            left = jnp.concatenate([lefts[u] for u in rows], axis=1)
            blocks = jnp.concatenate([near_v[table_s[e - u, i + u]] for u in rows], axis=0)
            collected_v[i + e] += nn(left, blocks)
        for u in range(HW):
            near_forward(i + u)

    loop(0, (clusters - 2 * HW) // HW, middle)

    @pl.when(me > 0)
    def _():
        edge_copy(True).wait_recv()

    @pl.when(me < devices - 1)
    def _():
        edge_copy(False).wait_recv()

    collected_v[HW : 2 * HW] += edge_in_v[1].astype(F32)
    collected_v[clusters : clusters + HW] += edge_in_v[0].astype(F32)

    loop(1, devices, lambda k: wide_arrival(k, slab_v, slab_v, slab_send, slab_recv).wait_recv())
    inputs[7].wait()
    inputs[8].wait()
    apex_right = jnp.zeros((rhs, lift_v.shape[1]), F32)
    apex_left = jnp.zeros((rhs, lift_v.shape[1]), F32)
    for t in range(slabs):
        other = jnp.where(my_slab == t, 0.0, 1.0)
        whole = jnp.concatenate([slab_v[t * leaves + j] for j in range(leaves)], axis=0)
        apex_right += other * three(whole[:rhs], apex_row_v[t], nt)
        apex_left += other * three(whole[rhs:], apex_col_v[t], nn)
    spread = three(jnp.concatenate([apex_right, apex_left], axis=0), lift_v[...], nt)

    loop(
        1,
        devices,
        lambda k: wide_arrival(k, parents_v, parents_v, parent_send, parent_recv).wait_recv(),
    )

    def far(f, total):
        live = jnp.where(f < count_s[0], 1.0, 0.0)
        ch, cl = split(coupling_v[f])
        chosen = parents_v[targets_s[f]]
        return total + live * (nt(chosen, ch) + nt(chosen, cl))

    def far_group(g, total):
        for u in range(unroll):
            total = far(g * unroll + u, total)
        return total

    far_right = lax.fori_loop(0, far_slots // unroll, far_group, spread[:rhs])

    loop(
        1, devices, lambda k: wide_arrival(k, outward_v, arrived_v, out_send, out_recv).wait_recv()
    )
    far_left = lax.fori_loop(
        0, devices, lambda d, total: total + arrived_v[d].astype(F32), spread[rhs:]
    )

    hat = jnp.concatenate([far_right, far_left], axis=0)
    hh, hl = split(hat)
    hat_both = jnp.concatenate([hh, hl], axis=0)

    def finish(c):
        th, tl = split(transfer_v[c])
        both = nt(hat_both, th)
        down = (both[: 2 * rhs] + both[2 * rhs :] + nt(hh, tl)).astype(BF)
        out = nn(down, basis_v[c])
        keep = lane < points_s[c]
        product_ref[:, window(c)] = jnp.where(keep, near_out_v[c] + out[:rhs], 0.0)
        adjoint_ref[:, window(c)] = jnp.where(keep, collected_v[c + HW] + out[rhs:], 0.0)

    def finish_group(g):
        for u in range(unroll):
            finish(g * unroll + u)

    loop(0, clusters // unroll, finish_group)

    loop(1, leaves, lambda k: share_copy(k).wait_send())
    loop(1, devices, lambda k: wide_copy(k, slab_v, slab_v, slab_send, slab_recv, False).wait_send())
    loop(
        1,
        devices,
        lambda k: wide_copy(k, parents_v, parents_v, parent_send, parent_recv, False).wait_send(),
    )
    loop(
        1,
        devices,
        lambda k: wide_copy(k, outward_v, arrived_v, out_send, out_recv, True).wait_send(),
    )

    @pl.when(me < devices - 1)
    def _():
        halo_copy(True).wait_send()
        edge_copy(True).wait_send()

    @pl.when(me > 0)
    def _():
        halo_copy(False).wait_send()
        edge_copy(False).wait_send()


def shards(
    right_sides,
    left_sides,
    near_blocks,
    near_columns,
    cluster_points,
    leaf_basis,
    transfer,
    far_parents,
    far_count,
    coupling,
    slab_transfer,
    apex_coupling,
):
    slabs, leaves = lax.axis_size("slab"), lax.axis_size("leaf")
    devices = slabs * leaves
    rhs, columns = right_sides.shape
    clusters, slots = near_columns.shape
    rank, k2 = transfer.shape[1:]
    k3 = slab_transfer.shape[2]
    width = 2 * HW + 1
    chunk = 2 * rhs // leaves
    smem = pl.BlockSpec(memory_space=pltpu.SMEM)
    hbm = pl.BlockSpec(memory_space=pltpu.HBM)
    vmem = pl.BlockSpec(memory_space=pltpu.VMEM)
    dma = pltpu.SemaphoreType.DMA
    out = jax.ShapeDtypeStruct((rhs, columns), F32)
    return pl.pallas_call(
        functools.partial(kernel, slabs, leaves),
        out_shape=(out, out),
        in_specs=[smem] * 3 + [hbm] * 9,
        out_specs=(vmem, vmem),
        scratch_shapes=[
            pltpu.VMEM((rhs, columns), BF),
            pltpu.VMEM((rhs, columns), BF),
            pltpu.VMEM(leaf_basis.shape, BF),
            pltpu.VMEM(transfer.shape, F32),
            pltpu.VMEM((k2, k3), F32),
            pltpu.VMEM(coupling.shape[1:], F32),
            pltpu.VMEM((slabs, k3, k3), F32),
            pltpu.VMEM((slabs, k3, k3), F32),
            pltpu.VMEM((clusters * slots + 1, B, B), BF),
            pltpu.VMEM((slots, clusters), jnp.int32),
            pltpu.VMEM((width + slots, clusters), jnp.int32),
            pltpu.VMEM((1, devices), jnp.int32),
            pltpu.SMEM((width + slots, clusters), jnp.int32),
            pltpu.SMEM((1, devices), jnp.int32),
            pltpu.VMEM((clusters + 2 * HW, rhs, B), BF),
            pltpu.VMEM((clusters, rhs, B), BF),
            pltpu.VMEM((clusters + 2 * HW, rhs, B), F32),
            pltpu.VMEM((clusters, rhs, B), F32),
            pltpu.VMEM((2, HW, rhs, B), BF),
            pltpu.VMEM((2, HW, rhs, B), BF),
            pltpu.VMEM((leaves, chunk, k3), F32),
            pltpu.VMEM((leaves, chunk, k3), F32),
            pltpu.VMEM((devices, chunk, k3), F32),
            pltpu.VMEM((devices, rhs, k2), BF),
            pltpu.VMEM((devices, rhs, k2), BF),
            pltpu.VMEM((devices, rhs, k2), BF),
            pltpu.VMEM((2 * rhs, rank), BF),
            dma((10,)),
            dma((2,)),
            dma((2,)),
            dma((2,)),
            dma((2,)),
            dma((2,)),
            dma((leaves,)),
            dma((leaves,)),
            dma((devices,)),
            dma((devices,)),
            dma((devices,)),
            dma((devices,)),
            dma((devices,)),
            dma((devices,)),
        ],
        compiler_params=pltpu.CompilerParams(
            collective_id=0, has_side_effects=True, vmem_limit_bytes=60 * 1024 * 1024
        ),
        name="h2_step",
    )(
        cluster_points,
        far_parents[0],
        far_count,
        near_columns.T,
        right_sides,
        left_sides,
        leaf_basis,
        transfer,
        slab_transfer[0],
        coupling[0],
        apex_coupling,
        near_blocks.reshape(-1, B, B),
    )


def solution(mesh):
    return jax.shard_map(
        shards,
        mesh=mesh,
        in_specs=(
            P(None, ("slab", "leaf")),
            P(None, ("slab", "leaf")),
            P(("slab", "leaf"), None, None, None),
            P(("slab", "leaf"), None),
            P(("slab", "leaf")),
            P(("slab", "leaf"), None, None),
            P(("slab", "leaf"), None, None),
            P(("slab", "leaf"), None),
            P(("slab", "leaf")),
            P(("slab", "leaf"), None, None, None),
            P(("slab", "leaf"), None, None),
            P(),
        ),
        out_specs=(P(None, ("slab", "leaf")), P(None, ("slab", "leaf"))),
        check_vma=False,
    )
```

```python
import functools

import jax
import jax.numpy as jnp
from jax import lax
from jax.experimental import pallas as pl
from jax.experimental.pallas import tpu as pltpu
from jax.sharding import PartitionSpec as P

B = 128
HW = 4
BF = jnp.bfloat16
F32 = jnp.float32
MESH = pl.DeviceIdType.MESH


def nt(a, b):
    return lax.dot_general(a, b, (((1,), (1,)), ((), ())), preferred_element_type=F32)


def nn(a, b):
    return lax.dot_general(a, b, (((1,), (0,)), ((), ())), preferred_element_type=F32)


def split(x):
    high = x.astype(BF)
    return high, (x - high.astype(F32)).astype(BF)


def three(a, b, product):
    rows = a.shape[0]
    ah, al = split(a)
    bh, bl = split(b)
    both = product(jnp.concatenate([ah, al], axis=0), bh)
    return both[:rows] + both[rows:] + product(ah, bl)


def kernel(
    slabs,
    leaves,
    points_s,
    targets_s,
    count_s,
    columns_h,
    right_h,
    left_h,
    basis_h,
    transfer_h,
    lift_h,
    coupling_h,
    apex_h,
    near_h,
    hat_ref,
    near_h_out,
    back_h_out,
    right_v,
    left_v,
    basis_v,
    transfer_v,
    lift_v,
    coupling_v,
    apex_row_v,
    apex_col_v,
    near_v,
    columns_v,
    table_v,
    far_table_v,
    table_s,
    far_table_s,
    ext_v,
    masked_left_v,
    collected_v,
    near_out_v,
    edge_out_v,
    edge_in_v,
    share_v,
    share_in_v,
    slab_v,
    parents_v,
    outward_v,
    arrived_v,
    in_sem,
    table_sem,
    halo_send,
    halo_recv,
    edge_send,
    edge_recv,
    share_send,
    share_recv,
    slab_send,
    slab_recv,
    parent_send,
    parent_recv,
    out_send,
    out_recv,
):
    rhs = right_h.shape[0]
    slots, clusters = columns_v.shape
    rank = basis_v.shape[1]
    far_slots = coupling_v.shape[0]
    devices = slabs * leaves
    width = 2 * HW + 1
    my_slab = lax.axis_index("slab")
    my_leaf = lax.axis_index("leaf")
    me = my_slab * leaves + my_leaf
    first = 1 - (me + devices - 1) // devices
    last = (me + 1) // devices

    def place(d):
        return (d // leaves, d % leaves)

    ext_v[0:HW] = jnp.zeros((HW, rhs, B), BF)
    ext_v[clusters + HW :] = jnp.zeros((HW, rhs, B), BF)
    edge_in_v[...] = jnp.zeros_like(edge_in_v)

    inputs = [
        pltpu.make_async_copy(src, dst, in_sem.at[i])
        for i, (src, dst) in enumerate(
            [
                (right_h, right_v),
                (left_h, left_v),
                (basis_h, basis_v),
                (transfer_h, transfer_v),
                (lift_h, lift_v),
                (coupling_h, coupling_v),
                (near_h, near_v.at[pl.ds(0, clusters * slots)]),
                (apex_h.at[my_slab], apex_row_v),
                (apex_h.at[:, my_slab], apex_col_v),
                (columns_h, columns_v),
            ]
        )
    ]
    inputs[9].start()
    for copy in inputs[:9]:
        copy.start()

    barrier = pltpu.get_barrier_semaphore()

    def greet(k, _):
        pl.semaphore_signal(
            barrier, inc=1, device_id=place((me + k) % devices), device_id_type=MESH
        )
        return 0

    lax.fori_loop(1, devices, greet, 0)

    collected_v[...] = jnp.zeros_like(collected_v)
    near_v[clusters * slots] = jnp.zeros((B, B), BF)

    inputs[9].wait()
    row = lax.broadcasted_iota(jnp.int32, (1, clusters), 1)
    opening = (
        row
        + first * jnp.maximum(HW - row, 0)
        - last * jnp.maximum(row - (clusters - HW - 1), 0)
    )
    spots = [columns_v[s : s + 1] - (me * clusters - HW) for s in range(slots)]
    for w in range(width):
        found = jnp.full((1, clusters), clusters * slots, jnp.int32)
        for s in range(slots):
            found = jnp.where(spots[s] == opening + w, row * slots + s, found)
        table_v[w : w + 1] = found
    for s in range(slots):
        table_v[width + s : width + s + 1] = jnp.clip(spots[s], 0, clusters + 2 * HW - 1)
    owner = lax.broadcasted_iota(jnp.int32, (1, devices), 1)
    found = jnp.full((1, devices), -1, jnp.int32)
    for f in range(far_slots):
        target = jnp.where(f < count_s[0], targets_s[f], -1)
        found = jnp.where(owner == target, f, found)
    far_table_v[0:1] = found
    tables = [
        pltpu.make_async_copy(table_v, table_s, table_sem.at[0]),
        pltpu.make_async_copy(far_table_v, far_table_s, table_sem.at[1]),
    ]
    for copy in tables:
        copy.start()

    for copy in inputs[:4]:
        copy.wait()

    lane = lax.broadcasted_iota(jnp.int32, (rhs, B), 1)

    def window(c):
        return pl.ds(pl.multiple_of(c * B, B), B)

    def mask_of(c):
        return jnp.where(lane < points_s[c], 1.0, 0.0)

    def leaf_step(c, total):
        mask = mask_of(c).astype(BF)
        r = right_v[:, window(c)] * mask
        l = left_v[:, window(c)] * mask
        ext_v[c + HW] = r
        masked_left_v[c] = l
        leaf = nt(jnp.concatenate([r, l], axis=0), basis_v[c])
        return total + three(leaf, transfer_v[c], nn)

    unroll = 4

    def leaf_group(g, total):
        for u in range(unroll):
            total = leaf_step(g * unroll + u, total)
        return total

    parent = lax.fori_loop(
        0, clusters // unroll, leaf_group, jnp.zeros((2 * rhs, transfer_v.shape[2]), F32)
    )

    parents_v[me] = parent[:rhs].astype(BF)
    inputs[4].wait()
    share = three(parent, lift_v[...], nn)
    chunk = share_v.shape[1]
    for j in range(leaves):
        share_v[j] = share[j * chunk : (j + 1) * chunk]

    pl.semaphore_wait(barrier, devices - 1)

    def halo_copy(to_next):
        where = me + 1 if to_next else me - 1
        src = clusters if to_next else HW
        dst = 0 if to_next else clusters + HW
        i = 0 if to_next else 1
        return pltpu.make_async_remote_copy(
            src_ref=ext_v.at[pl.ds(src, HW)],
            dst_ref=ext_v.at[pl.ds(dst, HW)],
            send_sem=halo_send.at[i],
            recv_sem=halo_recv.at[i],
            device_id=place(where),
            device_id_type=MESH,
        )

    def share_copy(k):
        peer = (my_leaf + k) % leaves
        return pltpu.make_async_remote_copy(
            src_ref=share_v.at[peer],
            dst_ref=share_in_v.at[my_leaf],
            send_sem=share_send.at[k],
            recv_sem=share_recv.at[k],
            device_id=(my_slab, peer),
            device_id_type=MESH,
        )

    def share_arrival(k):
        peer = (my_leaf + leaves - k) % leaves
        return pltpu.make_async_remote_copy(
            src_ref=share_v.at[my_leaf],
            dst_ref=share_in_v.at[peer],
            send_sem=share_send.at[k],
            recv_sem=share_recv.at[k],
            device_id=(my_slab, peer),
            device_id_type=MESH,
        )

    def wide_copy(k, src, dst, send, recv, spread):
        peer = (me + k) % devices
        return pltpu.make_async_remote_copy(
            src_ref=src.at[peer if spread else me],
            dst_ref=dst.at[me],
            send_sem=send.at[k],
            recv_sem=recv.at[k],
            device_id=place(peer),
            device_id_type=MESH,
        )

    def wide_arrival(k, src, dst, send, recv):
        peer = (me + devices - k) % devices
        return pltpu.make_async_remote_copy(
            src_ref=src.at[me],
            dst_ref=dst.at[peer],
            send_sem=send.at[k],
            recv_sem=recv.at[k],
            device_id=place(peer),
            device_id_type=MESH,
        )

    def loop(low, high, act):
        def step(k, carry):
            act(k)
            return carry

        lax.fori_loop(low, high, step, 0)

    loop(1, leaves, lambda k: share_copy(k).start())
    share_in_v[my_leaf] = share_v[my_leaf]

    @pl.when(me < devices - 1)
    def _():
        halo_copy(True).start()

    @pl.when(me > 0)
    def _():
        halo_copy(False).start()

    loop(
        1,
        devices,
        lambda k: wide_copy(k, parents_v, parents_v, parent_send, parent_recv, False).start(),
    )

    inputs[5].wait()
    for copy in tables:
        copy.wait()
    lh, ll = split(parent[rhs:])
    left_both = jnp.concatenate([lh, ll], axis=0)

    def outward(q):
        f = far_table_s[0, q]
        live = jnp.where(f >= 0, 1.0, 0.0)
        ch, cl = split(coupling_v[jnp.maximum(f, 0)])
        both = nn(left_both, ch)
        term = both[:rhs] + both[rhs:] + nn(lh, cl)
        outward_v[q] = (term * live).astype(BF)

    def outward_group(g):
        for u in range(unroll):
            outward(g * unroll + u)

    loop(0, devices // unroll, outward_group)
    arrived_v[me] = jnp.zeros((rhs, arrived_v.shape[2]), BF)

    loop(1, leaves, lambda k: share_arrival(k).wait_recv())
    total = share_in_v[0]
    for j in range(1, leaves):
        total = total + share_in_v[j]
    slab_v[me] = total

    loop(1, devices, lambda k: wide_copy(k, slab_v, slab_v, slab_send, slab_recv, False).start())
    loop(
        1,
        devices,
        lambda k: wide_copy(k, outward_v, arrived_v, out_send, out_recv, True).start(),
    )

    inputs[6].wait()

    def near_back(i, e0):
        left = masked_left_v[i]
        for w in range(width):
            collected_v[e0 + w] += nn(left, near_v[table_s[w, i]])

    def near_forward(i):
        blocks = jnp.concatenate([near_v[i * slots + s] for s in range(slots)], axis=1)
        picked = jnp.concatenate([ext_v[table_s[width + s, i]] for s in range(slots)], axis=1)
        near_out_v[i] = nt(picked, blocks)

    for i in range(HW):
        near_back(i, i + first * (HW - i))
    for i in range(clusters - HW, clusters):
        near_back(i, i - last * (i - (clusters - HW - 1)))

    edge_out_v[0] = collected_v[0:HW].astype(BF)
    edge_out_v[1] = collected_v[clusters + HW :].astype(BF)

    def edge_copy(to_next):
        i = 1 if to_next else 0
        return pltpu.make_async_remote_copy(
            src_ref=edge_out_v.at[i],
            dst_ref=edge_in_v.at[i],
            send_sem=edge_send.at[i],
            recv_sem=edge_recv.at[i],
            device_id=place(me + 1 if to_next else me - 1),
            device_id_type=MESH,
        )

    @pl.when(me < devices - 1)
    def _():
        edge_copy(True).start()

    @pl.when(me > 0)
    def _():
        edge_copy(False).start()

    @pl.when(me > 0)
    def _():
        halo_copy(True).wait_recv()

    @pl.when(me < devices - 1)
    def _():
        halo_copy(False).wait_recv()

    for i in list(range(HW)) + list(range(clusters - HW, clusters)):
        near_forward(i)

    def middle(g):
        i = HW + g * HW
        lefts = [masked_left_v[i + u] for u in range(HW)]
        for e in range(width + HW - 1):
            rows = [u for u in range(HW) if 0 <= e - u < width]
            left = jnp.concatenate([lefts[u] for u in rows], axis=1)
            blocks = jnp.concatenate([near_v[table_s[e - u, i + u]] for u in rows], axis=0)
            collected_v[i + e] += nn(left, blocks)
        for u in range(HW):
            near_forward(i + u)

    loop(0, (clusters - 2 * HW) // HW, middle)

    @pl.when(me > 0)
    def _():
        edge_copy(True).wait_recv()

    @pl.when(me < devices - 1)
    def _():
        edge_copy(False).wait_recv()

    collected_v[HW : 2 * HW] += edge_in_v[1].astype(F32)
    collected_v[clusters : clusters + HW] += edge_in_v[0].astype(F32)

    results = [
        pltpu.make_async_copy(near_out_v, near_h_out, table_sem.at[0]),
        pltpu.make_async_copy(
            collected_v.at[pl.ds(HW, clusters)], back_h_out, table_sem.at[1]
        ),
    ]
    for copy in results:
        copy.start()

    loop(1, devices, lambda k: wide_arrival(k, slab_v, slab_v, slab_send, slab_recv).wait_recv())
    inputs[7].wait()
    inputs[8].wait()
    apex_right = jnp.zeros((rhs, lift_v.shape[1]), F32)
    apex_left = jnp.zeros((rhs, lift_v.shape[1]), F32)
    for t in range(slabs):
        other = jnp.where(my_slab == t, 0.0, 1.0)
        whole = jnp.concatenate([slab_v[t * leaves + j] for j in range(leaves)], axis=0)
        apex_right += other * three(whole[:rhs], apex_row_v[t], nt)
        apex_left += other * three(whole[rhs:], apex_col_v[t], nn)
    spread = three(jnp.concatenate([apex_right, apex_left], axis=0), lift_v[...], nt)

    loop(
        1,
        devices,
        lambda k: wide_arrival(k, parents_v, parents_v, parent_send, parent_recv).wait_recv(),
    )

    def far(f, total):
        live = jnp.where(f < count_s[0], 1.0, 0.0)
        ch, cl = split(coupling_v[f])
        chosen = parents_v[targets_s[f]]
        return total + live * (nt(chosen, ch) + nt(chosen, cl))

    def far_group(g, total):
        for u in range(unroll):
            total = far(g * unroll + u, total)
        return total

    far_right = lax.fori_loop(0, far_slots // unroll, far_group, spread[:rhs])

    loop(
        1, devices, lambda k: wide_arrival(k, outward_v, arrived_v, out_send, out_recv).wait_recv()
    )
    far_left = lax.fori_loop(
        0, devices, lambda d, total: total + arrived_v[d].astype(F32), spread[rhs:]
    )

    hat_ref[:rhs] = far_right
    hat_ref[rhs:] = far_left
    for copy in results:
        copy.wait()

    loop(1, leaves, lambda k: share_copy(k).wait_send())
    loop(1, devices, lambda k: wide_copy(k, slab_v, slab_v, slab_send, slab_recv, False).wait_send())
    loop(
        1,
        devices,
        lambda k: wide_copy(k, parents_v, parents_v, parent_send, parent_recv, False).wait_send(),
    )
    loop(
        1,
        devices,
        lambda k: wide_copy(k, outward_v, arrived_v, out_send, out_recv, True).wait_send(),
    )

    @pl.when(me < devices - 1)
    def _():
        halo_copy(True).wait_send()
        edge_copy(True).wait_send()

    @pl.when(me > 0)
    def _():
        halo_copy(False).wait_send()
        edge_copy(False).wait_send()


def finish_kernel(
    points_s, hat_ref, transfer_ref, basis_ref, near_ref, back_ref, product_ref, adjoint_ref
):
    group = transfer_ref.shape[0]
    rhs = near_ref.shape[1]
    hh, hl = split(hat_ref[...])
    hat_both = jnp.concatenate([hh, hl], axis=0)
    lane = lax.broadcasted_iota(jnp.int32, (rhs, B), 1)
    for c in range(group):
        th, tl = split(transfer_ref[c])
        both = nt(hat_both, th)
        down = (both[: 2 * rhs] + both[2 * rhs :] + nt(hh, tl)).astype(BF)
        out = nn(down, basis_ref[c])
        keep = lane < points_s[pl.program_id(0) * group + c]
        columns = slice(c * B, (c + 1) * B)
        product_ref[:, columns] = jnp.where(keep, near_ref[c] + out[:rhs], 0.0)
        adjoint_ref[:, columns] = jnp.where(keep, back_ref[c] + out[rhs:], 0.0)


def shards(
    right_sides,
    left_sides,
    near_blocks,
    near_columns,
    cluster_points,
    leaf_basis,
    transfer,
    far_parents,
    far_count,
    coupling,
    slab_transfer,
    apex_coupling,
):
    slabs, leaves = lax.axis_size("slab"), lax.axis_size("leaf")
    devices = slabs * leaves
    rhs, columns = right_sides.shape
    clusters, slots = near_columns.shape
    rank, k2 = transfer.shape[1:]
    k3 = slab_transfer.shape[2]
    width = 2 * HW + 1
    chunk = 2 * rhs // leaves
    smem = pl.BlockSpec(memory_space=pltpu.SMEM)
    hbm = pl.BlockSpec(memory_space=pltpu.HBM)
    vmem = pl.BlockSpec(memory_space=pltpu.VMEM)
    dma = pltpu.SemaphoreType.DMA
    out = jax.ShapeDtypeStruct((rhs, columns), F32)
    blocks = jax.ShapeDtypeStruct((clusters, rhs, B), F32)
    hat, near_out, near_back = pl.pallas_call(
        functools.partial(kernel, slabs, leaves),
        out_shape=(jax.ShapeDtypeStruct((2 * rhs, k2), F32), blocks, blocks),
        in_specs=[smem] * 3 + [hbm] * 9,
        out_specs=(vmem, hbm, hbm),
        scratch_shapes=[
            pltpu.VMEM((rhs, columns), BF),
            pltpu.VMEM((rhs, columns), BF),
            pltpu.VMEM(leaf_basis.shape, BF),
            pltpu.VMEM(transfer.shape, F32),
            pltpu.VMEM((k2, k3), F32),
            pltpu.VMEM(coupling.shape[1:], F32),
            pltpu.VMEM((slabs, k3, k3), F32),
            pltpu.VMEM((slabs, k3, k3), F32),
            pltpu.VMEM((clusters * slots + 1, B, B), BF),
            pltpu.VMEM((slots, clusters), jnp.int32),
            pltpu.VMEM((width + slots, clusters), jnp.int32),
            pltpu.VMEM((1, devices), jnp.int32),
            pltpu.SMEM((width + slots, clusters), jnp.int32),
            pltpu.SMEM((1, devices), jnp.int32),
            pltpu.VMEM((clusters + 2 * HW, rhs, B), BF),
            pltpu.VMEM((clusters, rhs, B), BF),
            pltpu.VMEM((clusters + 2 * HW, rhs, B), F32),
            pltpu.VMEM((clusters, rhs, B), F32),
            pltpu.VMEM((2, HW, rhs, B), BF),
            pltpu.VMEM((2, HW, rhs, B), BF),
            pltpu.VMEM((leaves, chunk, k3), F32),
            pltpu.VMEM((leaves, chunk, k3), F32),
            pltpu.VMEM((devices, chunk, k3), F32),
            pltpu.VMEM((devices, rhs, k2), BF),
            pltpu.VMEM((devices, rhs, k2), BF),
            pltpu.VMEM((devices, rhs, k2), BF),
            dma((10,)),
            dma((2,)),
            dma((2,)),
            dma((2,)),
            dma((2,)),
            dma((2,)),
            dma((leaves,)),
            dma((leaves,)),
            dma((devices,)),
            dma((devices,)),
            dma((devices,)),
            dma((devices,)),
            dma((devices,)),
            dma((devices,)),
        ],
        compiler_params=pltpu.CompilerParams(
            collective_id=0, has_side_effects=True, vmem_limit_bytes=60 * 1024 * 1024
        ),
        name="h2_step",
    )(
        cluster_points,
        far_parents[0],
        far_count,
        near_columns.T,
        right_sides,
        left_sides,
        leaf_basis,
        transfer,
        slab_transfer[0],
        coupling[0],
        apex_coupling,
        near_blocks.reshape(-1, B, B),
    )
    group = 8
    return pl.pallas_call(
        finish_kernel,
        out_shape=(out, out),
        grid=(clusters // group,),
        in_specs=[
            smem,
            pl.BlockSpec((2 * rhs, k2), lambda g: (0, 0)),
            pl.BlockSpec((group, rank, k2), lambda g: (g, 0, 0)),
            pl.BlockSpec((group, rank, B), lambda g: (g, 0, 0)),
            pl.BlockSpec((group, rhs, B), lambda g: (g, 0, 0)),
            pl.BlockSpec((group, rhs, B), lambda g: (g, 0, 0)),
        ],
        out_specs=(
            pl.BlockSpec((rhs, group * B), lambda g: (0, g)),
            pl.BlockSpec((rhs, group * B), lambda g: (0, g)),
        ),
        name="h2_finish",
    )(cluster_points, hat, transfer, leaf_basis, near_out, near_back)


def solution(mesh):
    return jax.shard_map(
        shards,
        mesh=mesh,
        in_specs=(
            P(None, ("slab", "leaf")),
            P(None, ("slab", "leaf")),
            P(("slab", "leaf"), None, None, None),
            P(("slab", "leaf"), None),
            P(("slab", "leaf")),
            P(("slab", "leaf"), None, None),
            P(("slab", "leaf"), None, None),
            P(("slab", "leaf"), None),
            P(("slab", "leaf")),
            P(("slab", "leaf"), None, None, None),
            P(("slab", "leaf"), None, None),
            P(),
        ),
        out_specs=(P(None, ("slab", "leaf")), P(None, ("slab", "leaf"))),
        check_vma=False,
    )
```
